128 devices in a mesh: row: 32 (over z, y, core), col: 4 (over x).
Axes of the slice: x: 4, y: 4, z: 4, core: 2. Of those that a mesh axis runs over, the one named last changes fastest.
Arguments:
- matrix: float32 [24576, 16384], P('row', 'col'), may hold values from -6 to 6
Outputs:
- updated: float32 [24576, 16384], P('row', 'col')
The draws below stay inside these ranges and needn't reach their ends.
All inputs are finite; a program needn't handle non-finite values.
Results may differ from the reference program's by a relative error of at most 0.0003.
Values sent between devices are 32-bit elements; how exact they have to be, the bound alone decides.
No kernel may reach another device: no remote copies, remote signals or barrier semaphores. Data moves between devices by JAX's collectives and lax.ppermute only.
A program may use at most 128 MiB of HBM per device.

```python
import jax
import jax.numpy as jnp
from jax import lax

PANEL = 128
N = 16384
M = 24576


def block_scale(rng, dims, split, least, high):
    loudness, own = 1.0, jax.random.fold_in(rng, 6)
    for axis_at, shards_of in split:
        steps = jnp.exp(jax.random.uniform(jax.random.fold_in(own, axis_at), (shards_of,), jnp.float32, least / len(split), high / len(split)))
        loudness = loudness * jnp.repeat(steps, dims[axis_at] // shards_of).reshape([-1 if axis == axis_at else 1 for axis in range(len(dims))])
    return loudness


def gaussian(own_key, extent, spread, most, cuts=(), kind=jnp.bfloat16):
    drawn = jax.random.normal(own_key, extent, jnp.float32) * spread
    if len(cuts) > 0:
        drawn = block_scale(own_key, extent, cuts, -0.22, 0.18) * drawn
    return jnp.clip(drawn, min=-most, max=most).astype(kind)


def setup_inputs(seed: int = 0) -> dict:
    key_list = jax.random.split(jax.random.key(seed), 2)
    matrix = gaussian(key_list[0], (M, N), 1.0, 6.0, ((0, 32), (1, 4)), jnp.float32)
    return dict(matrix=matrix)


def eliminate(working):
    count = working.shape[0]
    positions = jnp.arange(count).astype(jnp.int32)

    def one_column(column, state):
        pivot_value = state[column, column]
        below = positions > column
        multiplier = jnp.where(below, state[:, column] / pivot_value, jnp.zeros_like(state[:, column]))
        pivot_row = jnp.where(below, state[column, :], jnp.zeros_like(state[column, :]))
        state = state - multiplier[:, None] * pivot_row[None, :]
        return state.at[:, column].set(jnp.where(below, multiplier, state[:, column]))
    result = lax.fori_loop(0, count, one_column, working)
    lower_unit = jnp.tril(result, -1) + jnp.eye(count, dtype=result.dtype)
    upper_tri = jnp.triu(result)
    return (lower_unit, upper_tri)

def reference(matrix):
    high = lax.Precision.HIGHEST
    panel_cols = matrix[:, :PANEL]
    orthonormal, triangle = jnp.linalg.qr(panel_cols)
    sign_fix = jnp.sign(jnp.diagonal(triangle))
    orthonormal = orthonormal * sign_fix[None, :]
    lower_unit, upper_tri = eliminate(orthonormal[:PANEL] + jnp.eye(PANEL, dtype=jnp.float32))
    reflectors = jax.scipy.linalg.solve_triangular(upper_tri.T, orthonormal.T, lower=True)
    reflectors = reflectors.at[:, :PANEL].set(lower_unit.T)
    projected = jnp.dot(reflectors, matrix, precision=high)
    coefficients = jax.scipy.linalg.solve_triangular(lower_unit, jnp.dot(upper_tri.T, projected, precision=high), lower=True, unit_diagonal=True)
    return matrix - jnp.dot(reflectors.T, coefficients, precision=high)
```

```python
import functools

import jax
import jax.numpy as jnp
from jax import lax
from jax.experimental import pallas as pl
from jax.experimental.pallas import tpu as pltpu
from jax.sharding import PartitionSpec as P

PANEL = 128
HIGH = lax.Precision.HIGHEST
F32 = jnp.float32
BF16 = jnp.bfloat16
VMEM_BYTES = 48 << 20


def row_of(z, y, c):
    return (z * 4 + y) * 2 + c


def axis_pairs(which, step, keep=lambda z, y, c: True):
    pairs = []
    for z in range(4):
        for y in range(4):
            for c in range(2):
                if not keep(z, y, c):
                    continue
                if (c == 0) == (which == 0):
                    to = row_of(z, (y + step) % 4, c)
                else:
                    to = row_of((z + step) % 4, y, c)
                pairs.append((row_of(z, y, c), to))
    return pairs


CORE_PAIRS = [(r, r ^ 1) for r in range(32)]


def first(x, step):
    return lax.ppermute(x, "row", axis_pairs(0, step))


def second(x, step):
    return lax.ppermute(x, "row", axis_pairs(1, step))


def swap(x):
    return lax.ppermute(x, "row", CORE_PAIRS)


def dot3(x, y):
    return jnp.dot(x, y, preferred_element_type=F32)


def split(x):
    high = x.astype(BF16)
    return high, (x - high.astype(F32)).astype(BF16)


def params():
    return pltpu.CompilerParams(vmem_limit_bytes=VMEM_BYTES)


def coords(r, half):
    y, z = (r // 2) % 4, r // 8
    return jnp.where(half == 0, y, z), jnp.where(half == 0, z, y)


def panel_kernel(r_ref, a_ref, pa_ref, pb_ref, keep_ref, send_ref):
    r = r_ref[0]
    panel = a_ref[...]
    rows = panel.shape[0] // 2
    pa_ref[...] = panel[:rows]
    pb_ref[...] = panel[rows:]
    gram = lax.dot_general(panel, panel, (((0,), (0,)), ((), ())), precision=HIGH, preferred_element_type=F32)
    top = jnp.where(r == 0, panel[:PANEL], 0.0)
    even = r % 2 == 0
    keep_ref[...] = jnp.where(even, gram, top)
    send_ref[...] = jnp.where(even, top, gram)


def panel_call(r, a):
    rows = a.shape[0]
    half = jax.ShapeDtypeStruct((rows // 2, PANEL), F32)
    square = jax.ShapeDtypeStruct((PANEL, PANEL), F32)
    whole = lambda shape: pl.BlockSpec(shape, lambda i, r: (0,) * len(shape))
    return pl.pallas_call(
        panel_kernel,
        grid_spec=pltpu.PrefetchScalarGridSpec(
            num_scalar_prefetch=1,
            grid=(1,),
            in_specs=[pl.BlockSpec((rows, PANEL), lambda i, r: (0, 0))],
            out_specs=[whole((rows // 2, PANEL))] * 2 + [whole((PANEL, PANEL))] * 2,
        ),
        out_shape=[half, half, square, square],
        compiler_params=params(),
        name="panel",
    )(r, a)


def top_kernel(a_ref, lower_ref, upper_ref):
    for k in range(16):
        lower_ref[k] = a_ref[:, k * PANEL : (k + 1) * PANEL]
        upper_ref[k] = a_ref[:, (k + 16) * PANEL : (k + 17) * PANEL]


def top_call(a):
    cols = a.shape[1]
    out = jax.ShapeDtypeStruct((16, PANEL, PANEL), F32)
    return pl.pallas_call(
        top_kernel,
        grid=(1,),
        in_specs=[pl.BlockSpec((PANEL, cols), lambda i: (0, 0))],
        out_specs=[pl.BlockSpec((16, PANEL, PANEL), lambda i: (0, 0, 0))] * 2,
        out_shape=[out, out],
        compiler_params=params(),
        name="top_rows",
    )(a)


def pick_panel(x, pa, pb, ra1, ra2, rb1, rb2):
    upper = jnp.where(x == 0, pa[...], jnp.where(x == 1, ra1[...], ra2[...]))
    lower = jnp.where(x == 0, pb[...], jnp.where(x == 3, rb1[...], rb2[...]))
    return jnp.concatenate([upper, lower], axis=0)


def product_steps(s_ref, a_ref, lhs, out_ref):
    half = s_ref[2]
    _, b0 = coords(s_ref[0], half)
    high, low = split(a_ref[...])
    both = dot3(lhs, high)
    result = both[:PANEL] + both[PANEL:] + dot3(lhs[:PANEL], low)
    for b in range(4):
        out_ref[(b - b0 + 4) % 4] = result[:, b * PANEL : (b + 1) * PANEL]


def product_first_kernel(s_ref, a_ref, pa, pb, ra1, ra2, rb1, rb2, out_ref, lhs_ref, panel_ref):
    @pl.when(pl.program_id(0) == 0)
    def _():
        panel = pick_panel(s_ref[1], pa, pb, ra1, ra2, rb1, rb2)
        panel_ref[...] = panel
        high, low = split(panel.T)
        lhs_ref[:PANEL] = high
        lhs_ref[PANEL:] = low

    product_steps(s_ref, a_ref, lhs_ref[...], out_ref)


def product_second_kernel(s_ref, a_ref, lhs_ref, out_ref):
    product_steps(s_ref, a_ref, lhs_ref[...], out_ref)


def piece_map(i, s_ref):
    half = s_ref[2]
    a0, _ = coords(s_ref[0], half)
    return (0, half * 4 + (a0 + i) % 4)


def product_call(scalars, a, panels=None, lhs=None):
    rows = a.shape[0]
    whole = lambda shape: pl.BlockSpec(shape, lambda i, s: (0,) * len(shape))
    a_spec = pl.BlockSpec((rows, 512), piece_map)
    w_spec = pl.BlockSpec((4, PANEL, PANEL), lambda i, s: (i, 0, 0))
    w_shape = jax.ShapeDtypeStruct((16, PANEL, PANEL), F32)
    if lhs is None:
        return pl.pallas_call(
            product_first_kernel,
            grid_spec=pltpu.PrefetchScalarGridSpec(
                num_scalar_prefetch=1,
                grid=(4,),
                in_specs=[a_spec] + [whole((rows // 2, PANEL))] * 6,
                out_specs=[w_spec, whole((2 * PANEL, rows)), whole((rows, PANEL))],
            ),
            out_shape=[
                w_shape,
                jax.ShapeDtypeStruct((2 * PANEL, rows), BF16),
                jax.ShapeDtypeStruct((rows, PANEL), F32),
            ],
            compiler_params=params(),
            name="product_first",
        )(scalars, a, *panels)
    return pl.pallas_call(
        product_second_kernel,
        grid_spec=pltpu.PrefetchScalarGridSpec(
            num_scalar_prefetch=1,
            grid=(4,),
            in_specs=[a_spec, whole((2 * PANEL, rows))],
            out_specs=w_spec,
        ),
        out_shape=w_shape,
        compiler_params=params(),
        name="product_second",
    )(scalars, a, lhs)


def eliminate_steps(blocks, full):
    lane = lax.broadcasted_iota(jnp.int32, (8, PANEL), 1)
    sub = lax.broadcasted_iota(jnp.int32, (8, PANEL), 0)
    for k in range(PANEL):
        at, off = k // 8, k % 8
        row = blocks[at][off : off + 1, :]
        inverse = 1.0 / row[:, k : k + 1]
        here = lane == k
        scaled = jnp.where(here[:1], inverse, row * inverse)
        spread = jnp.broadcast_to(scaled, (8, PANEL))
        for i in range(0 if full else at, 16):
            col = jnp.broadcast_to(blocks[i][:, k : k + 1], (8, PANEL))
            new = jnp.where(here, 0.0, blocks[i]) - col * spread
            if i == at:
                if full:
                    new = jnp.where(sub == off, spread, new)
                else:
                    new = jnp.where(sub > off, new, blocks[i])
            blocks[i] = new
    return blocks


def factor_kernel(r_ref, g_ref, other_ref, out_ref):
    even = r_ref[0] % 2 == 0
    gram = jnp.where(even, g_ref[...], other_ref[...])
    blocks = eliminate_steps([gram[8 * i : 8 * i + 8] for i in range(16)], False)
    lane = lax.broadcasted_iota(jnp.int32, (8, PANEL), 1)
    sub = lax.broadcasted_iota(jnp.int32, (8, PANEL), 0)
    for i in range(16):
        at = sub + 8 * i
        pivot = jnp.sum(jnp.where(lane == at, blocks[i], 0.0), axis=1, keepdims=True)
        scale = lax.rsqrt(pivot)
        unit = jnp.where(lane < at, blocks[i], jnp.where(lane == at, 1.0, 0.0))
        out_ref[8 * i : 8 * i + 8] = unit * scale


SMEM_SPEC = pl.BlockSpec(memory_space=pltpu.SMEM)


def small_call(kernel, out_shape, name, *args):
    vmem = pl.BlockSpec(memory_space=pltpu.VMEM)
    return pl.pallas_call(
        kernel,
        in_specs=[SMEM_SPEC] + [vmem] * (len(args) - 1),
        out_specs=vmem,
        out_shape=out_shape,
        compiler_params=params(),
        name=name,
    )(*args)


def basis_kernel(r_ref, linv_ref, g_ref, other_ref, panel_ref, out_ref):
    even = r_ref[0] % 2 == 0
    top = jnp.where(even, other_ref[...], g_ref[...])
    linv = linv_ref[...]
    nt = (((1,), (1,)), ((), ()))
    q_top = lax.dot_general(top, linv, nt, precision=HIGH, preferred_element_type=F32)
    lane = lax.broadcasted_iota(jnp.int32, (8, PANEL), 1)
    sub = lax.broadcasted_iota(jnp.int32, (8, PANEL), 0)
    blocks = [q_top[8 * i : 8 * i + 8] + jnp.where(lane == sub + 8 * i, 1.0, 0.0) for i in range(16)]
    kinv = jnp.concatenate(eliminate_steps(blocks, True), axis=0)
    tn = (((0,), (0,)), ((), ()))
    change = lax.dot_general(linv, kinv, tn, precision=HIGH, preferred_element_type=F32)
    basis = jnp.dot(panel_ref[...], change, precision=HIGH, preferred_element_type=F32)
    rest = basis[PANEL:]
    upper = basis[:PANEL] + jnp.where(r_ref[0] == 0, kinv, 0.0)
    for part, begin, end in ((upper, 0, PANEL), (rest, PANEL, basis.shape[0])):
        high, low = split(part)
        out_ref[begin:end, 0:PANEL] = high
        out_ref[begin:end, PANEL : 2 * PANEL] = low
        out_ref[begin:end, 2 * PANEL :] = high


def shard_kernel(r_ref, linv_ref, top_ref, w0, w1, w2, w3, out_ref):
    w = w0[...] + w1[...] + w2[...] + w3[...]
    out_ref[...] = jnp.dot(linv_ref[...], w, precision=HIGH, preferred_element_type=F32) + top_ref[...]


def update_kernel(s_ref, a_ref, v_ref, z0, z1, z2, z3, *rest):
    out_ref = rest[-1]
    half = s_ref[2]
    _, b0 = coords(s_ref[0], half)
    for i, z_ref in enumerate((z0, z1, z2, z3)):

        @pl.when(pl.program_id(0) == i)
        def _(z_ref=z_ref):
            for b in range(4):
                high, low = split(z_ref[(b0 - b + 4) % 4])
                stacked = jnp.concatenate([high, high, low], axis=0)
                cols = slice(b * PANEL, (b + 1) * PANEL)
                out_ref[:, cols] = a_ref[:, cols] - dot3(v_ref[...], stacked)


def gather_map(i, s_ref):
    half = s_ref[2]
    a0, _ = coords(s_ref[0], half)
    return (0, half * 4 + (a0 - i + 4) % 4)


def update_call(scalars, a, v, pieces, out=None):
    rows, cols = a.shape
    whole = lambda shape: pl.BlockSpec(shape, lambda i, s: (0,) * len(shape))
    extra, extra_specs, alias = (), [], {}
    if out is not None:
        extra, extra_specs, alias = (out,), [pl.BlockSpec(memory_space=pl.ANY)], {7: 0}
    return pl.pallas_call(
        update_kernel,
        grid_spec=pltpu.PrefetchScalarGridSpec(
            num_scalar_prefetch=1,
            grid=(4,),
            in_specs=[pl.BlockSpec((rows, 512), gather_map), whole((rows, 3 * PANEL))]
            + [whole((4, PANEL, PANEL))] * 4
            + extra_specs,
            out_specs=pl.BlockSpec((rows, 512), gather_map),
        ),
        out_shape=jax.ShapeDtypeStruct((rows, cols), F32),
        input_output_aliases=alias,
        compiler_params=params(),
        name="update",
    )(scalars, a, v, *pieces, *extra)


def on_device(a):
    r = lax.axis_index("row").astype(jnp.int32)
    x = lax.axis_index("col").astype(jnp.int32)
    r1 = r.reshape(1)
    core = r % 2
    own = jnp.stack([r, x, core])
    other = jnp.stack([r, x, 1 - core])

    pa, pb, keep, send = panel_call(r1, a)
    ra1 = lax.ppermute(pa, "col", [(0, 1)])
    rb1 = lax.ppermute(pb, "col", [(0, 3)])
    rb2 = lax.ppermute(jnp.where(x == 0, pb, rb1), "col", [(0, 1), (3, 2)])
    ra2 = lax.ppermute(jnp.where(x == 0, pa, ra1), "col", [(0, 3), (1, 2)])

    g = keep + swap(send)
    g = g + first(g, 1) + first(g, 2) + first(g, 3)
    g = g + second(g, 1) + second(g, 2) + second(g, 3)
    away = [lax.ppermute(g, "col", [(0, s)]) for s in (1, 2, 3)]
    g = jnp.where(x == 0, g, away[0] + away[1] + away[2])
    g_other = swap(g)

    lower, upper = top_call(a)
    upper = lax.ppermute(upper, "row", [(0, 1)])
    mine = jnp.where(core == 0, lower, upper)
    top = mine[0:4]
    corner = lambda z, y, c: z == 0 and y == 0
    for s in (1, 2, 3):
        got = lax.ppermute(mine[4 * s : 4 * s + 4], "row", axis_pairs(0, s, corner))
        top = jnp.where((jnp.where(core == 0, (r // 2) % 4, r // 8)) == s, got, top)
    edge = lambda z, y, c: (z if c == 0 else y) == 0
    shard_top = top[0]
    for t in (1, 2, 3):
        got = lax.ppermute(top[t], "row", axis_pairs(1, t, edge))
        shard_top = jnp.where((jnp.where(core == 0, r // 8, (r // 2) % 4)) == t, got, shard_top)

    w_other, lhs, panel = product_call(other, a, panels=(pa, pb, ra1, ra2, rb1, rb2))
    w_got = swap(w_other)
    w_own = product_call(own, a, lhs=lhs)
    w = [w_own[4 * s : 4 * s + 4] + w_got[4 * s : 4 * s + 4] for s in range(4)]
    w = w[0] + first(w[1], 1) + first(w[2], 2) + first(w[3], 3)
    w = [w[0]] + [second(w[t], t) for t in (1, 2, 3)]

    square = jax.ShapeDtypeStruct((PANEL, PANEL), F32)
    linv = small_call(factor_kernel, square, "factor", r1, g, g_other)
    z = small_call(shard_kernel, square, "shard", r1, linv, shard_top, *w)

    z = jnp.stack([z] + [second(z, t) for t in (1, 2, 3)])
    pieces = [z] + [first(z, s) for s in (1, 2, 3)]
    got = [swap(piece) for piece in pieces]

    stacked = jax.ShapeDtypeStruct((a.shape[0], 3 * PANEL), BF16)
    v = small_call(basis_kernel, stacked, "basis", r1, linv, g, g_other, panel)
    out = update_call(own, a, v, pieces)
    return update_call(other, a, v, got, out)


def solution(mesh):
    return jax.shard_map(
        on_device, mesh=mesh, in_specs=(P("row", "col"),), out_specs=P("row", "col"), check_vma=False
    )
```

```python
import functools

import jax
import jax.numpy as jnp
from jax import lax
from jax.experimental import pallas as pl
from jax.experimental.pallas import tpu as pltpu
from jax.sharding import PartitionSpec as P

PANEL = 128
WIDTH = 512
LARGE = 52
HIGH = lax.Precision.HIGHEST
F32 = jnp.float32
BF16 = jnp.bfloat16


def near(a):
    return a ^ 1


def far(a):
    return 3 - a


def row_of(z, y, c):
    return (z * 4 + y) * 2 + c


def axis_pairs(which, step, keep=lambda a, b: True):
    pairs = []
    for z in range(4):
        for y in range(4):
            for c in range(2):
                a, b = (z, y) if c else (y, z)
                if keep(a, b):
                    to = (step(a), b) if which == 0 else (a, step(b))
                    tz, ty = to if c else to[::-1]
                    pairs.append((row_of(z, y, c), row_of(tz, ty, c)))
    return pairs


def along(which, step, x, keep=lambda a, b: True):
    return lax.ppermute(x, "row", axis_pairs(which, step, keep))


def swap(x):
    return lax.ppermute(x, "row", [(r, r ^ 1) for r in range(32)])


def piece_at(a0, i):
    return jnp.where(i == 0, a0, jnp.where(i == 1, far(a0), jnp.where(i == 2, near(a0), a0 ^ 2)))


def dot3(x, y):
    return jnp.dot(x, y, preferred_element_type=F32)


def split(x):
    high = x.astype(BF16)
    return high, (x - high.astype(F32)).astype(BF16)


def params(mib):
    return pltpu.CompilerParams(vmem_limit_bytes=mib << 20)


def cost_of(microseconds):
    return pl.CostEstimate(flops=int(microseconds * 1.15e9), bytes_accessed=0, transcendentals=0)


def small_call(kernel, shapes, name, *args, scratch=(), mib=8, after=(), cost=None, hbm=0):
    vmem = pl.BlockSpec(memory_space=pltpu.VMEM)
    shapes = [shape if isinstance(shape[0], tuple) else (shape, F32) for shape in shapes]
    return pl.pallas_call(
        kernel,
        in_specs=[pl.BlockSpec(memory_space=pltpu.HBM)] * hbm
        + [vmem] * (len(args) - hbm)
        + [pl.BlockSpec(memory_space=pl.ANY)] * len(after),
        out_specs=[vmem] * len(shapes),
        out_shape=[jax.ShapeDtypeStruct(*shape) for shape in shapes],
        scratch_shapes=scratch,
        compiler_params=params(mib),
        cost_estimate=cost,
        name=name,
    )(*args, *after)


def place(flip=False):
    r = lax.axis_index("row")
    z, y, core = r >> 3, (r >> 1) & 3, r & 1
    if flip:
        core = 1 - core
    return core, jnp.where(core == 0, y, z), jnp.where(core == 0, z, y)


def panel_kernel(a_ref, pa_ref, pb_ref, sem):
    rows = pa_ref.shape[0]
    copies = [
        pltpu.make_async_copy(a_ref.at[i * rows : (i + 1) * rows, :PANEL], out_ref, sem.at[i])
        for i, out_ref in enumerate((pa_ref, pb_ref))
    ]
    for copy in copies:
        copy.start()
    for copy in copies:
        copy.wait()


def panel_call(a):
    half = jax.ShapeDtypeStruct((a.shape[0] // 2, PANEL), F32)
    return pl.pallas_call(
        panel_kernel,
        in_specs=[pl.BlockSpec(memory_space=pltpu.HBM)],
        out_specs=[pl.BlockSpec(memory_space=pltpu.VMEM)] * 2,
        out_shape=[half, half],
        scratch_shapes=[pltpu.SemaphoreType.DMA((2,))],
        compiler_params=params(LARGE),
        name="panel",
    )(a)


def top_kernel(a_ref, lower_ref, upper_ref, rows_ref, sem):
    copy = pltpu.make_async_copy(a_ref.at[:PANEL], rows_ref, sem)
    copy.start()
    copy.wait()
    for half, out_ref in enumerate((lower_ref, upper_ref)):
        for i, piece in enumerate((0, 3, 1, 2)):
            for j, shard in enumerate((0, 3, 1, 2)):
                begin = (4 * half + piece) * WIDTH + shard * PANEL
                out_ref[4 * i + j] = rows_ref[:, begin : begin + PANEL]


def top_call(a):
    scratch = [pltpu.VMEM((PANEL, a.shape[1]), F32), pltpu.SemaphoreType.DMA]
    keys = dict(scratch=scratch, mib=LARGE, hbm=1, cost=cost_of(1.5))
    return small_call(top_kernel, [(16, PANEL, PANEL)] * 2, "top_rows", a, **keys)


def load_kernel(a_ref, blocks_ref, sem):
    copies = []
    for i in range(8):
        source = a_ref.at[:, i * WIDTH : (i + 1) * WIDTH]
        copies.append(pltpu.make_async_copy(source, blocks_ref.at[i], sem.at[i]))
        copies[i].start()
    for copy in copies:
        copy.wait()


def load_call(a):
    scratch = [pltpu.SemaphoreType.DMA((8,))]
    keys = dict(scratch=scratch, mib=36, hbm=1, cost=cost_of(5))
    return small_call(load_kernel, [(8, a.shape[0], WIDTH)], "load", a, **keys)[0]


def share_kernel(index, below, mine_ref, got_ref, keep_ref, send_ref):
    count = keep_ref.shape[0]
    held = place()[index] < below

    @pl.when(held)
    def _():
        keep_ref[...] = mine_ref[:count]
        send_ref[...] = mine_ref[count:]

    @pl.when(jnp.logical_not(held))
    def _():
        keep_ref[...] = got_ref[:count]
        send_ref[...] = got_ref[count:]


def share(index, below, mine, got):
    shape = (mine.shape[0] // 2, PANEL, PANEL)
    return small_call(functools.partial(share_kernel, index, below), [shape] * 2, "share", mine, got)


def pick_panel(pa, pb, a01, a03, a12, b01, b03, b32):
    x = lax.axis_index("col")
    upper = jnp.where(x == 0, pa[...], jnp.where(x == 1, a01[...], jnp.where(x == 2, a12[...], a03[...])))
    lower = jnp.where(x == 0, pb[...], jnp.where(x == 1, b01[...], jnp.where(x == 2, b32[...], b03[...])))
    return jnp.concatenate([upper, lower], axis=0)


def product_steps(flip, a_ref, lhs_ref, out_ref):
    half, a0, _ = place(flip)
    for i in range(4):
        high, low = split(a_ref[half * 4 + piece_at(a0, i)])
        both = dot3(lhs_ref[...], high)
        out_ref[i] = both[:PANEL] + both[PANEL:] + dot3(lhs_ref[:PANEL], low)


def product_first_kernel(a_ref, *refs):
    out_ref, lhs_ref, panel_ref, keep_ref, send_ref = refs[-5:]
    r = lax.axis_index("row")
    panel = pick_panel(*refs[:8])
    panel_ref[...] = panel
    flipped = panel.T
    high, low = split(flipped)
    lhs_ref[:PANEL] = high
    lhs_ref[PANEL:] = low
    gram = jnp.dot(flipped, panel, precision=HIGH, preferred_element_type=F32)
    top = jnp.where(r == 0, panel[:PANEL], 0.0)
    even = r & 1 == 0
    keep_ref[...] = jnp.where(even, gram, top)
    send_ref[...] = jnp.where(even, top, gram)
    product_steps(True, a_ref, lhs_ref, out_ref)


def product_second_kernel(a_ref, lhs_ref, out_ref):
    product_steps(False, a_ref, lhs_ref, out_ref)


def product_call(blocks, panels=None, lhs=None):
    rows = blocks.shape[1]
    w = ((4, PANEL, WIDTH), F32)
    if lhs is not None:
        return small_call(product_second_kernel, [w], "product_second", blocks, lhs, mib=24, cost=cost_of(1.5))[0]
    square = ((PANEL, PANEL), F32)
    shapes = [w, ((2 * PANEL, rows), BF16), ((rows, PANEL), F32), square, square]
    return small_call(product_first_kernel, shapes, "product_first", blocks, *panels, mib=24, cost=cost_of(2))


def spread(x, j):
    return jnp.broadcast_to(x[:, j : j + 1], (8, PANEL))


def tree_sum(terms):
    while len(terms) > 1:
        odd = [terms[-1]] if len(terms) % 2 else []
        terms = [p + q for p, q in zip(terms[::2], terms[1::2])] + odd
    return terms[0]


def chol_blocks(blocks):
    lane = lax.broadcasted_iota(jnp.int32, (8, PANEL), 1)
    sub = lax.broadcasted_iota(jnp.int32, (8, PANEL), 0)
    done = []
    for p in range(16):
        at = 8 * p
        rows = [jnp.broadcast_to(blocks[p][j : j + 1], (8, PANEL)) for j in range(8)]
        d = [[spread(rows[i], at + j) for j in range(i + 1)] for i in range(8)]
        t = [[None] * 8 for _ in range(8)]
        for k in range(8):
            r = lax.rsqrt(d[k][k])
            low = {i: d[i][k] * r for i in range(k + 1, 8)}
            for j in range(k):
                t[k][j] = t[k][j] * r
            t[k][k] = r
            for i in range(k + 1, 8):
                for j in range(k + 1, i + 1):
                    d[i][j] = d[i][j] - low[i] * low[j]
                for j in range(k + 1):
                    step = low[i] * t[k][j]
                    t[i][j] = -step if t[i][j] is None else t[i][j] - step
        inside = (lane >= at) & (lane < at + 8)
        rows = [jnp.where(inside, jnp.where(lane == at + j, 1.0, 0.0), rows[j]) for j in range(8)]
        y = []
        for i in range(8):
            terms = [t[i][j] * rows[j] for j in range(i + 1)]
            y.append(tree_sum(terms))
        out = y[0]
        for i in range(1, 8):
            out = jnp.where(sub == i, y[i], out)
        done.append(jnp.where(lane < at + 8, out, 0.0))
        if p == 15:
            break
        xs = []
        for k in range(8):
            terms = [t[i][k] * y[i] for i in range(k, 8)]
            xs.append(tree_sum(terms))
        for i in range(p + 1, 16):
            terms = [spread(blocks[i], at + k) * xs[k] for k in range(8)]
            blocks[i] = jnp.where(inside, 0.0, blocks[i]) - tree_sum(terms)
    return done


def inverse_blocks(blocks):
    lane = lax.broadcasted_iota(jnp.int32, (8, PANEL), 1)
    sub = lax.broadcasted_iota(jnp.int32, (8, PANEL), 0)
    for p in range(16):
        at = 8 * p
        rows = [jnp.broadcast_to(blocks[p][j : j + 1], (8, PANEL)) for j in range(8)]
        d = [[spread(rows[i], at + j) for j in range(8)] for i in range(8)]
        for k in range(8):
            r = 1.0 / d[k][k]
            row = [r if j == k else d[k][j] * r for j in range(8)]
            for i in range(8):
                if i != k:
                    m = d[i][k]
                    d[i] = [-(m * row[j]) if j == k else d[i][j] - m * row[j] for j in range(8)]
            d[k] = row
        inside = (lane >= at) & (lane < at + 8)
        rows = [jnp.where(inside, jnp.where(lane == at + j, 1.0, 0.0), rows[j]) for j in range(8)]
        xs = []
        for k in range(8):
            terms = [d[k][j] * rows[j] for j in range(8)]
            xs.append(tree_sum(terms))
        new = []
        for i in range(16):
            if i == p:
                out = xs[0]
                for k in range(1, 8):
                    out = jnp.where(sub == k, xs[k], out)
                new.append(out)
                continue
            terms = [spread(blocks[i], at + k) * xs[k] for k in range(8)]
            new.append(jnp.where(inside, 0.0, blocks[i]) - tree_sum(terms))
        blocks = new
    return blocks


def factor_kernel(g_ref, other_ref, w_ref, top_ref, got_ref, out_ref, z_ref):
    core, _, b0 = place()
    gram = jnp.where(core == 0, g_ref[...], other_ref[...])
    blocks = chol_blocks([gram[8 * i : 8 * i + 8] for i in range(16)])
    for i in range(16):
        out_ref[8 * i : 8 * i + 8] = blocks[i]
    top = jnp.where(b0 < 2, top_ref[0], got_ref[0])
    z_ref[...] = jnp.dot(out_ref[...], w_ref[...], precision=HIGH, preferred_element_type=F32) + top


def basis_kernel(linv_ref, g_ref, other_ref, panel_ref, out_ref):
    core, _, _ = place()
    top = jnp.where(core == 0, other_ref[...], g_ref[...])
    linv = linv_ref[...]
    nt = (((1,), (1,)), ((), ()))
    q_top = lax.dot_general(top, linv, nt, precision=HIGH, preferred_element_type=F32)
    lane = lax.broadcasted_iota(jnp.int32, (8, PANEL), 1)
    sub = lax.broadcasted_iota(jnp.int32, (8, PANEL), 0)
    blocks = [q_top[8 * i : 8 * i + 8] + jnp.where(lane == sub + 8 * i, 1.0, 0.0) for i in range(16)]
    kinv = jnp.concatenate(inverse_blocks(blocks), axis=0)
    tn = (((0,), (0,)), ((), ()))
    change = lax.dot_general(linv, kinv, tn, precision=HIGH, preferred_element_type=F32)
    basis = jnp.dot(panel_ref[...], change, precision=HIGH, preferred_element_type=F32)
    rest = basis[PANEL:]
    upper = basis[:PANEL] + jnp.where(lax.axis_index("row") == 0, kinv, 0.0)
    for part, begin, end in ((upper, 0, PANEL), (rest, PANEL, basis.shape[0])):
        high, low = split(part)
        out_ref[begin:end, 0:PANEL] = high
        out_ref[begin:end, PANEL : 2 * PANEL] = low
        out_ref[begin:end, 2 * PANEL :] = high


def cores_kernel(own_ref, got_ref, keep_ref, kept_ref, *out_refs):
    gram = keep_ref[...] + kept_ref[...]
    for i, out_ref in enumerate(out_refs):
        out_ref[:, :WIDTH] = own_ref[i] + got_ref[i]
        out_ref[:, WIDTH:] = gram


def first_kernel(e0, e1, e2, e3, *refs):
    out_refs, shards = refs[:4], refs[4]
    total = e0[...] + e1[...] + e2[...] + e3[...]
    for t in range(4):
        shards[t] = total[:, t * PANEL : (t + 1) * PANEL]
    _, _, b0 = place()
    for i, out_ref in enumerate(out_refs):
        out_ref[:, :PANEL] = shards[piece_at(b0, i)]
        out_ref[:, PANEL:] = total[:, WIDTH:]


def second_kernel(e0, e1, e2, e3, w_ref, g_ref):
    total = e0[...] + e1[...] + e2[...] + e3[...]
    w_ref[...] = total[:, :PANEL]
    g_ref[...] = total[:, PANEL:]


def assemble_kernel(z0, z1, z2, z3, out_ref):
    _, _, b0 = place()
    for i, z_ref in enumerate((z0, z1, z2, z3)):
        out_ref[piece_at(b0, i)] = z_ref[...]


def update_kernel(count, begin, a_ref, v_ref, *refs):
    z_refs = refs[: 2 * count]
    out_ref, token_ref, buffer, sem = refs[-4:]
    token_ref[...] = jnp.zeros_like(token_ref)
    writes = []
    for i in range(2 * count):
        half, a0, _ = place(i >= count)
        piece = half * 4 + piece_at(a0, begin + i % count)
        cols = pl.ds(pl.multiple_of(piece * WIDTH, WIDTH), WIDTH)
        parts = [split(z_refs[i][t]) for t in range(4)]
        high = jnp.concatenate([part[0] for part in parts], axis=1)
        low = jnp.concatenate([part[1] for part in parts], axis=1)
        stacked = jnp.concatenate([high, high, low], axis=0)
        buffer[i] = a_ref[piece] - dot3(v_ref[...], stacked)
        writes.append(pltpu.make_async_copy(buffer.at[i], out_ref.at[:, cols], sem.at[i]))
        writes[i].start()
    for write in writes:
        write.wait()


def update_call(blocks, v, mine, theirs, begin, out=None):
    _, rows, width = blocks.shape
    count = len(mine)
    vmem = pl.BlockSpec(memory_space=pltpu.VMEM)
    extra = () if out is None else (out,)
    return pl.pallas_call(
        functools.partial(update_kernel, count, begin),
        in_specs=[vmem] * (2 + 2 * count) + [pl.BlockSpec(memory_space=pltpu.HBM)] * len(extra),
        out_specs=[pl.BlockSpec(memory_space=pltpu.HBM), vmem],
        out_shape=[jax.ShapeDtypeStruct((rows, 8 * width), F32), jax.ShapeDtypeStruct((8, PANEL), F32)],
        input_output_aliases={2 + 2 * count: 0} if extra else {},
        scratch_shapes=[pltpu.VMEM((2 * count, rows, WIDTH), F32), pltpu.SemaphoreType.DMA((2 * count,))],
        compiler_params=params(28),
        name="update",
    )(blocks, v, *mine, *theirs, *extra)


def hold_kernel(*refs):
    pass


def hold(arrays, after):
    anywhere = pl.BlockSpec(memory_space=pl.ANY)
    return pl.pallas_call(
        hold_kernel,
        in_specs=[anywhere] * (len(arrays) + 1),
        out_specs=[anywhere] * len(arrays),
        out_shape=[jax.ShapeDtypeStruct(array.shape, array.dtype) for array in arrays],
        input_output_aliases={i: i for i in range(len(arrays))},
        compiler_params=params(2),
        name="hold",
    )(*arrays, after)


def diagonal(a):
    return a ^ 2


STEPS = (far, near, diagonal)


def on_device(a):
    rows = a.shape[0]
    pa, pb = panel_call(a)
    a01 = lax.ppermute(pa, "col", [(0, 1)])
    b03 = lax.ppermute(pb, "col", [(0, 3)])
    b01 = lax.ppermute(pb, "col", [(0, 1)])
    a03 = lax.ppermute(pa, "col", [(0, 3)])
    a12 = lax.ppermute(a01, "col", [(1, 2)])
    b32 = lax.ppermute(b03, "col", [(3, 2)])

    lower, upper = top_call(a)
    upper = lax.ppermute(upper, "row", [(0, 1)])
    top, send = share(0, 1, lower, upper)
    got = along(0, near, send, lambda a, b: a == 0 and b == 0)
    top, send = share(1, 1, top, got)
    got = along(0, far, send, lambda a, b: a < 2 and b == 0)
    top, send = share(1, 2, top, got)
    got = along(1, near, send, lambda a, b: b == 0)
    top, send = share(2, 1, top, got)
    got = along(1, far, send, lambda a, b: b < 2)

    blocks = load_call(a)
    w_other, lhs, panel, keep, send = product_call(blocks, panels=(pa, pb, a01, a03, a12, b01, b03, b32))
    w_got, kept = swap(w_other), swap(send)
    w_own = product_call(blocks, lhs=lhs)
    e = small_call(cores_kernel, [(PANEL, WIDTH + PANEL)] * 4, "sum_cores", w_own, w_got, keep, kept)
    e = [e[0]] + [along(0, step, e[i + 1]) for i, step in enumerate(STEPS)]
    scratch = [pltpu.VMEM((4, PANEL, PANEL), F32)]
    e = small_call(first_kernel, [(PANEL, 2 * PANEL)] * 4, "sum_first", *e, scratch=scratch)
    e = [e[0]] + [along(1, step, e[i + 1]) for i, step in enumerate(STEPS)]
    w, g = small_call(second_kernel, [(PANEL, PANEL)] * 2, "sum_second", *e)
    g_other = swap(g)
    linv, z = small_call(factor_kernel, [(PANEL, PANEL)] * 2, "factor", g, g_other, w, top, got, cost=cost_of(5))

    z = [z] + [along(1, step, z) for step in STEPS]
    (z,) = small_call(assemble_kernel, [(4, PANEL, PANEL)], "assemble", *z)
    got = [along(0, step, z) for step in STEPS]
    theirs = swap(z)
    shapes = [((rows, 3 * PANEL), BF16)]
    (v,) = small_call(basis_kernel, shapes, "basis", linv, g, g_other, panel, mib=16, cost=cost_of(7))
    out, token = update_call(blocks, v, [z], [theirs], 0)
    got = hold(got, token)
    theirs = [swap(piece) for piece in got]
    out, _ = update_call(blocks, v, got[:2], theirs[:2], 1, out)
    out, _ = update_call(blocks, v, got[2:], theirs[2:], 3, out)
    return out


def solution(mesh):
    return jax.shard_map(
        on_device, mesh=mesh, in_specs=(P("row", "col"),), out_specs=P("row", "col"), check_vma=False
    )
```

```python
import functools

import jax
import jax.numpy as jnp
from jax import lax
from jax.experimental import pallas as pl
from jax.experimental.pallas import tpu as pltpu
from jax.sharding import PartitionSpec as P

PANEL = 128
WIDTH = 512
LARGE = 52
HIGH = lax.Precision.HIGHEST
F32 = jnp.float32
BF16 = jnp.bfloat16


def near(a):
    return a ^ 1


def far(a):
    return 3 - a


def diagonal(a):
    return a ^ 2


STEPS = (far, near, diagonal)


def row_of(z, y, c):
    return (z * 4 + y) * 2 + c


def axis_pairs(which, step, keep=lambda a, b: True):
    pairs = []
    for z in range(4):
        for y in range(4):
            for c in range(2):
                a, b = (z, y) if c else (y, z)
                if keep(a, b):
                    to = (step(a), b) if which == 0 else (a, step(b))
                    tz, ty = to if c else to[::-1]
                    pairs.append((row_of(z, y, c), row_of(tz, ty, c)))
    return pairs


def along(which, step, x, keep=lambda a, b: True):
    return lax.ppermute(x, "row", axis_pairs(which, step, keep))


def swap(x):
    return lax.ppermute(x, "row", [(r, r ^ 1) for r in range(32)])


def piece_at(a0, i):
    return jnp.where(i == 0, a0, jnp.where(i == 1, far(a0), jnp.where(i == 2, near(a0), a0 ^ 2)))


def dot3(x, y):
    return jnp.dot(x, y, preferred_element_type=F32)


def split(x):
    high = x.astype(BF16)
    return high, (x - high.astype(F32)).astype(BF16)


def params(mib):
    return pltpu.CompilerParams(vmem_limit_bytes=mib << 20)


def cost_of(microseconds):
    return pl.CostEstimate(flops=int(microseconds * 1.15e9), bytes_accessed=0, transcendentals=0)


def small_call(kernel, shapes, name, *args, scratch=(), mib=8, after=(), cost=None, hbm=0):
    vmem = pl.BlockSpec(memory_space=pltpu.VMEM)
    shapes = [shape if isinstance(shape[0], tuple) else (shape, F32) for shape in shapes]
    return pl.pallas_call(
        kernel,
        in_specs=[pl.BlockSpec(memory_space=pltpu.HBM)] * hbm
        + [vmem] * (len(args) - hbm)
        + [pl.BlockSpec(memory_space=pl.ANY)] * len(after),
        out_specs=[vmem] * len(shapes),
        out_shape=[jax.ShapeDtypeStruct(*shape) for shape in shapes],
        scratch_shapes=scratch,
        compiler_params=params(mib),
        cost_estimate=cost,
        name=name,
    )(*args, *after)


def place(flip=False):
    r = lax.axis_index("row")
    z, y, core = r >> 3, (r >> 1) & 3, r & 1
    if flip:
        core = 1 - core
    return core, jnp.where(core == 0, y, z), jnp.where(core == 0, z, y)


def panel_kernel(a_ref, pa_ref, pb_ref, sem):
    rows = pa_ref.shape[0]
    copies = [
        pltpu.make_async_copy(a_ref.at[i * rows : (i + 1) * rows, :PANEL], out_ref, sem.at[i])
        for i, out_ref in enumerate((pa_ref, pb_ref))
    ]
    for copy in copies:
        copy.start()
    for copy in copies:
        copy.wait()


def panel_call(a):
    half = jax.ShapeDtypeStruct((a.shape[0] // 2, PANEL), F32)
    return pl.pallas_call(
        panel_kernel,
        in_specs=[pl.BlockSpec(memory_space=pltpu.HBM)],
        out_specs=[pl.BlockSpec(memory_space=pltpu.VMEM)] * 2,
        out_shape=[half, half],
        scratch_shapes=[pltpu.SemaphoreType.DMA((2,))],
        compiler_params=params(LARGE),
        name="panel",
    )(a)


def load_kernel(a_ref, blocks_ref, lower_ref, upper_ref, sem):
    copies = []
    for i in range(8):
        source = a_ref.at[:, i * WIDTH : (i + 1) * WIDTH]
        copies.append(pltpu.make_async_copy(source, blocks_ref.at[i], sem.at[i]))
        copies[i].start()
    for copy in copies:
        copy.wait()

    @pl.when(lax.axis_index("row") == 0)
    def _():
        for i, piece in enumerate((0, 3, 1, 2)):
            lower_ref[i] = blocks_ref[piece, :PANEL]
            upper_ref[i] = blocks_ref[piece + 4, :PANEL]


def load_call(a):
    scratch = [pltpu.SemaphoreType.DMA((8,))]
    keys = dict(scratch=scratch, mib=36, hbm=1, cost=cost_of(5))
    top = (4, PANEL, WIDTH)
    return small_call(load_kernel, [(8, a.shape[0], WIDTH), top, top], "load", a, **keys)


def split_kernel(lower_ref, upper_ref, *out_refs):
    core, _, _ = place()
    for i, out_ref in enumerate(out_refs):

        @pl.when(core == 0)
        def _(i=i, out_ref=out_ref):
            out_ref[...] = lower_ref[i]

        @pl.when(core != 0)
        def _(i=i, out_ref=out_ref):
            out_ref[...] = upper_ref[i]


def pick_kernel(mine_ref, far_ref, near_ref, diagonal_ref, out_ref):
    _, a0, _ = place()
    for at, ref in ((0, mine_ref), (far(0), far_ref), (near(0), near_ref), (diagonal(0), diagonal_ref)):

        @pl.when(a0 == at)
        def _(ref=ref):
            out_ref[...] = ref[...]


def pick_panel(pa, pb, a01, a03, a12, b01, b03, b32):
    x = lax.axis_index("col")
    upper = jnp.where(x == 0, pa[...], jnp.where(x == 1, a01[...], jnp.where(x == 2, a12[...], a03[...])))
    lower = jnp.where(x == 0, pb[...], jnp.where(x == 1, b01[...], jnp.where(x == 2, b32[...], b03[...])))
    return jnp.concatenate([upper, lower], axis=0)


def product_steps(flip, a_ref, lhs_ref, out_ref):
    half, a0, _ = place(flip)
    for i in range(4):
        high, low = split(a_ref[half * 4 + piece_at(a0, i)])
        both = dot3(lhs_ref[...], high)
        out_ref[i] = both[:PANEL] + both[PANEL:] + dot3(lhs_ref[:PANEL], low)


def product_first_kernel(a_ref, *refs):
    out_ref, lhs_ref, panel_ref, keep_ref, send_ref = refs[-5:]
    r = lax.axis_index("row")
    panel = pick_panel(*refs[:8])
    panel_ref[...] = panel
    flipped = panel.T
    high, low = split(flipped)
    lhs_ref[:PANEL] = high
    lhs_ref[PANEL:] = low
    gram = jnp.dot(flipped, panel, precision=HIGH, preferred_element_type=F32)
    top = jnp.where(r == 0, panel[:PANEL], 0.0)
    even = r & 1 == 0
    keep_ref[...] = jnp.where(even, gram, top)
    send_ref[...] = jnp.where(even, top, gram)
    product_steps(True, a_ref, lhs_ref, out_ref)


def product_second_kernel(a_ref, lhs_ref, out_ref):
    product_steps(False, a_ref, lhs_ref, out_ref)


def product_call(blocks, panels=None, lhs=None, after=()):
    rows = blocks.shape[1]
    w = ((4, PANEL, WIDTH), F32)
    if lhs is not None:
        return small_call(product_second_kernel, [w], "product_second", blocks, lhs, mib=24, cost=cost_of(1.5))[0]
    square = ((PANEL, PANEL), F32)
    shapes = [w, ((2 * PANEL, rows), BF16), ((rows, PANEL), F32), square, square]
    return small_call(product_first_kernel, shapes, "product_first", blocks, *panels, mib=24, cost=cost_of(2), after=after)


def spread(x, j):
    return jnp.broadcast_to(x[:, j : j + 1], (8, PANEL))


def tree_sum(terms):
    while len(terms) > 1:
        odd = [terms[-1]] if len(terms) % 2 else []
        terms = [p + q for p, q in zip(terms[::2], terms[1::2])] + odd
    return terms[0]


def chol_blocks(blocks):
    lane = lax.broadcasted_iota(jnp.int32, (8, PANEL), 1)
    sub = lax.broadcasted_iota(jnp.int32, (8, PANEL), 0)
    done = []
    for p in range(16):
        at = 8 * p
        rows = [jnp.broadcast_to(blocks[p][j : j + 1], (8, PANEL)) for j in range(8)]
        d = [[spread(rows[i], at + j) for j in range(i + 1)] for i in range(8)]
        t = [[None] * 8 for _ in range(8)]
        for k in range(8):
            r = lax.rsqrt(d[k][k])
            low = {i: d[i][k] * r for i in range(k + 1, 8)}
            for j in range(k):
                t[k][j] = t[k][j] * r
            t[k][k] = r
            for i in range(k + 1, 8):
                for j in range(k + 1, i + 1):
                    d[i][j] = d[i][j] - low[i] * low[j]
                for j in range(k + 1):
                    step = low[i] * t[k][j]
                    t[i][j] = -step if t[i][j] is None else t[i][j] - step
        inside = (lane >= at) & (lane < at + 8)
        rows = [jnp.where(inside, jnp.where(lane == at + j, 1.0, 0.0), rows[j]) for j in range(8)]
        y = []
        for i in range(8):
            terms = [t[i][j] * rows[j] for j in range(i + 1)]
            y.append(tree_sum(terms))
        out = y[0]
        for i in range(1, 8):
            out = jnp.where(sub == i, y[i], out)
        done.append(jnp.where(lane < at + 8, out, 0.0))
        if p == 15:
            break
        xs = []
        for k in range(8):
            terms = [t[i][k] * y[i] for i in range(k, 8)]
            xs.append(tree_sum(terms))
        for i in range(p + 1, 16):
            terms = [spread(blocks[i], at + k) * xs[k] for k in range(8)]
            blocks[i] = jnp.where(inside, 0.0, blocks[i]) - tree_sum(terms)
    return done


def inverse_blocks(blocks):
    lane = lax.broadcasted_iota(jnp.int32, (8, PANEL), 1)
    sub = lax.broadcasted_iota(jnp.int32, (8, PANEL), 0)
    for p in range(16):
        at = 8 * p
        rows = [jnp.broadcast_to(blocks[p][j : j + 1], (8, PANEL)) for j in range(8)]
        d = [[spread(rows[i], at + j) for j in range(8)] for i in range(8)]
        for k in range(8):
            r = 1.0 / d[k][k]
            row = [r if j == k else d[k][j] * r for j in range(8)]
            for i in range(8):
                if i != k:
                    m = d[i][k]
                    d[i] = [-(m * row[j]) if j == k else d[i][j] - m * row[j] for j in range(8)]
            d[k] = row
        inside = (lane >= at) & (lane < at + 8)
        rows = [jnp.where(inside, jnp.where(lane == at + j, 1.0, 0.0), rows[j]) for j in range(8)]
        xs = []
        for k in range(8):
            terms = [d[k][j] * rows[j] for j in range(8)]
            xs.append(tree_sum(terms))
        new = []
        for i in range(16):
            if i == p:
                out = xs[0]
                for k in range(1, 8):
                    out = jnp.where(sub == k, xs[k], out)
                new.append(out)
                continue
            terms = [spread(blocks[i], at + k) * xs[k] for k in range(8)]
            new.append(jnp.where(inside, 0.0, blocks[i]) - tree_sum(terms))
        blocks = new
    return blocks


def factor_kernel(g_ref, other_ref, out_ref):
    core, _, _ = place()
    gram = jnp.where(core == 0, g_ref[...], other_ref[...])
    blocks = chol_blocks([gram[8 * i : 8 * i + 8] for i in range(16)])
    for i in range(16):
        out_ref[8 * i : 8 * i + 8] = blocks[i]


def basis_kernel(linv_ref, g_ref, other_ref, panel_ref, out_ref):
    core, _, _ = place()
    top = jnp.where(core == 0, other_ref[...], g_ref[...])
    linv = linv_ref[...]
    nt = (((1,), (1,)), ((), ()))
    q_top = lax.dot_general(top, linv, nt, precision=HIGH, preferred_element_type=F32)
    lane = lax.broadcasted_iota(jnp.int32, (8, PANEL), 1)
    sub = lax.broadcasted_iota(jnp.int32, (8, PANEL), 0)
    blocks = [q_top[8 * i : 8 * i + 8] + jnp.where(lane == sub + 8 * i, 1.0, 0.0) for i in range(16)]
    kinv = jnp.concatenate(inverse_blocks(blocks), axis=0)
    tn = (((0,), (0,)), ((), ()))
    change = lax.dot_general(linv, kinv, tn, precision=HIGH, preferred_element_type=F32)
    basis = jnp.dot(panel_ref[...], change, precision=HIGH, preferred_element_type=F32)
    rest = basis[PANEL:]
    upper = basis[:PANEL] + jnp.where(lax.axis_index("row") == 0, kinv, 0.0)
    for part, begin, end in ((upper, 0, PANEL), (rest, PANEL, basis.shape[0])):
        high, low = split(part)
        out_ref[begin:end, 0:PANEL] = high
        out_ref[begin:end, PANEL : 2 * PANEL] = low
        out_ref[begin:end, 2 * PANEL :] = high


def cores_kernel(own_ref, got_ref, keep_ref, kept_ref, *out_refs):
    gram = keep_ref[...] + kept_ref[...]
    for i, out_ref in enumerate(out_refs):
        out_ref[:, :WIDTH] = own_ref[i] + got_ref[i]
        out_ref[:, WIDTH:] = gram


def first_kernel(e0, e1, e2, e3, after_ref, w_ref, g_ref):
    total = e0[...] + e1[...] + e2[...] + e3[...]
    w_ref[...] = total[:, :WIDTH]
    g_ref[...] = total[:, WIDTH:]


def gram_kernel(g0, g1, g2, g3, *refs):
    out_ref = refs[-1]
    out_ref[...] = g0[...] + g1[...] + g2[...] + g3[...]


def piece_kernel(linv_ref, w0, w1, w2, w3, mine_ref, far_ref, near_ref, diagonal_ref, out_ref):
    _, _, b0 = place()
    w = w0[...] + w1[...] + w2[...] + w3[...]
    z = jnp.dot(linv_ref[...], w, precision=HIGH, preferred_element_type=F32)
    for at, ref in ((0, mine_ref), (far(0), far_ref), (near(0), near_ref), (diagonal(0), diagonal_ref)):

        @pl.when(b0 == at)
        def _(ref=ref):
            out_ref[...] = z + ref[...]


def update_kernel(count, begin, a_ref, v_ref, *refs):
    z_refs = refs[: 2 * count]
    out_ref, buffer, sem = refs[-3:]
    writes = []
    for i in range(2 * count):
        half, a0, _ = place(i >= count)
        piece = half * 4 + piece_at(a0, begin + i % count)
        cols = pl.ds(pl.multiple_of(piece * WIDTH, WIDTH), WIDTH)
        high, low = split(z_refs[i][...])
        stacked = jnp.concatenate([high, high, low], axis=0)
        buffer[i] = a_ref[piece] - dot3(v_ref[...], stacked)
        writes.append(pltpu.make_async_copy(buffer.at[i], out_ref.at[:, cols], sem.at[i]))
        writes[i].start()
    for write in writes:
        write.wait()


def update_call(blocks, v, mine, theirs, begin, out=None):
    _, rows, width = blocks.shape
    count = len(mine)
    vmem = pl.BlockSpec(memory_space=pltpu.VMEM)
    extra = () if out is None else (out,)
    return pl.pallas_call(
        functools.partial(update_kernel, count, begin),
        in_specs=[vmem] * (2 + 2 * count) + [pl.BlockSpec(memory_space=pltpu.HBM)] * len(extra),
        out_specs=pl.BlockSpec(memory_space=pltpu.HBM),
        out_shape=jax.ShapeDtypeStruct((rows, 8 * width), F32),
        input_output_aliases={2 + 2 * count: 0} if extra else {},
        scratch_shapes=[pltpu.VMEM((2 * count, rows, WIDTH), F32), pltpu.SemaphoreType.DMA((2 * count,))],
        compiler_params=params(32),
        name="update",
    )(blocks, v, *mine, *theirs, *extra)


def hold_kernel(*refs):
    pass


def hold(arrays, after):
    anywhere = pl.BlockSpec(memory_space=pl.ANY)
    return pl.pallas_call(
        hold_kernel,
        in_specs=[anywhere] * (len(arrays) + 1),
        out_specs=[anywhere] * len(arrays),
        out_shape=[jax.ShapeDtypeStruct(array.shape, array.dtype) for array in arrays],
        input_output_aliases={i: i for i in range(len(arrays))},
        compiler_params=params(2),
        name="hold",
    )(*arrays, after)


def on_device(a):
    rows = a.shape[0]
    pa, pb = panel_call(a)
    a01 = lax.ppermute(pa, "col", [(0, 1)])
    b03 = lax.ppermute(pb, "col", [(0, 3)])
    b01 = lax.ppermute(pb, "col", [(0, 1)])
    a03 = lax.ppermute(pa, "col", [(0, 3)])
    a12 = lax.ppermute(a01, "col", [(1, 2)])
    b32 = lax.ppermute(b03, "col", [(3, 2)])

    blocks, lower, upper = load_call(a)
    upper = lax.ppermute(upper, "row", [(0, 1)])
    tops = small_call(split_kernel, [(PANEL, WIDTH)] * 4, "split", lower, upper)
    got = [along(0, step, tops[i + 1], lambda a, b: a == 0 and b == 0) for i, step in enumerate(STEPS)]
    (top,) = small_call(pick_kernel, [(PANEL, WIDTH)], "pick", tops[0], *got)
    tops = [top] + [along(1, step, top, lambda a, b: b == 0) for step in STEPS]

    w_other, lhs, panel, keep, send_g = product_call(blocks, panels=(pa, pb, a01, a03, a12, b01, b03, b32))
    w_got, kept = swap(w_other), swap(send_g)
    w_own = product_call(blocks, lhs=lhs)
    e = small_call(cores_kernel, [(PANEL, WIDTH + PANEL)] * 4, "sum_cores", w_own, w_got, keep, kept)
    e = [e[0]] + [along(0, step, e[i + 1]) for i, step in enumerate(STEPS)]
    w, g = small_call(first_kernel, [(PANEL, WIDTH), (PANEL, PANEL)], "sum_first", *e, after=(top,))
    g = [g] + [along(1, step, g) for step in STEPS]
    w = [w] + [along(1, step, w) for step in STEPS]
    (g,) = small_call(gram_kernel, [(PANEL, PANEL)], "sum_gram", *g, after=tops[1:], cost=cost_of(3))
    g_other = swap(g)
    (linv,) = small_call(factor_kernel, [(PANEL, PANEL)], "factor", g, g_other, cost=cost_of(0.5))
    (z,) = small_call(piece_kernel, [(PANEL, WIDTH)], "piece", linv, *w, *tops)

    got = [along(0, step, z) for step in STEPS]
    theirs = swap(z)
    shapes = [((rows, 3 * PANEL), BF16)]
    (v,) = small_call(basis_kernel, shapes, "basis", linv, g, g_other, panel, mib=16, cost=cost_of(7))
    got = hold(got, v)
    others = [swap(piece) for piece in got]
    out = update_call(blocks, v, [z], [theirs], 0)
    return update_call(blocks, v, got, others, 1, out)


def solution(mesh):
    return jax.shard_map(
        on_device, mesh=mesh, in_specs=(P("row", "col"),), out_specs=P("row", "col"), check_vma=False
    )
```

```python
import functools

import jax
import jax.numpy as jnp
from jax import lax
from jax.experimental import pallas as pl
from jax.experimental.pallas import tpu as pltpu
from jax.sharding import PartitionSpec as P

PANEL = 128
WIDTH = 512
LARGE = 52
HIGH = lax.Precision.HIGHEST
F32 = jnp.float32
BF16 = jnp.bfloat16


def near(a):
    return a ^ 1


def far(a):
    return 3 - a


def diagonal(a):
    return a ^ 2


STEPS = (far, near, diagonal)


def row_of(z, y, c):
    return (z * 4 + y) * 2 + c


def axis_pairs(which, step, keep=lambda a, b: True):
    pairs = []
    for z in range(4):
        for y in range(4):
            for c in range(2):
                a, b = (z, y) if c else (y, z)
                if keep(a, b):
                    to = (step(a), b) if which == 0 else (a, step(b))
                    tz, ty = to if c else to[::-1]
                    pairs.append((row_of(z, y, c), row_of(tz, ty, c)))
    return pairs


def along(which, step, x, keep=lambda a, b: True):
    return lax.ppermute(x, "row", axis_pairs(which, step, keep))


def swap(x):
    return lax.ppermute(x, "row", [(r, r ^ 1) for r in range(32)])


def piece_at(a0, i):
    return jnp.where(i == 0, a0, jnp.where(i == 1, far(a0), jnp.where(i == 2, near(a0), a0 ^ 2)))


def dot3(x, y):
    return jnp.dot(x, y, preferred_element_type=F32)


def split(x):
    high = x.astype(BF16)
    return high, (x - high.astype(F32)).astype(BF16)


def params(mib):
    return pltpu.CompilerParams(vmem_limit_bytes=mib << 20)


def cost_of(microseconds):
    return pl.CostEstimate(flops=int(microseconds * 1.15e9), bytes_accessed=0, transcendentals=0)


def small_call(kernel, shapes, name, *args, scratch=(), mib=8, after=(), cost=None, hbm=0):
    vmem = pl.BlockSpec(memory_space=pltpu.VMEM)
    shapes = [shape if isinstance(shape[0], tuple) else (shape, F32) for shape in shapes]
    return pl.pallas_call(
        kernel,
        in_specs=[pl.BlockSpec(memory_space=pltpu.HBM)] * hbm
        + [vmem] * (len(args) - hbm)
        + [pl.BlockSpec(memory_space=pl.ANY)] * len(after),
        out_specs=[vmem] * len(shapes),
        out_shape=[jax.ShapeDtypeStruct(*shape) for shape in shapes],
        scratch_shapes=scratch,
        compiler_params=params(mib),
        cost_estimate=cost,
        name=name,
    )(*args, *after)


def place(flip=False):
    r = lax.axis_index("row")
    z, y, core = r >> 3, (r >> 1) & 3, r & 1
    if flip:
        core = 1 - core
    return core, jnp.where(core == 0, y, z), jnp.where(core == 0, z, y)


def panel_kernel(a_ref, pa_ref, pb_ref, sem):
    rows = pa_ref.shape[0]
    copies = [
        pltpu.make_async_copy(a_ref.at[i * rows : (i + 1) * rows, :PANEL], out_ref, sem.at[i])
        for i, out_ref in enumerate((pa_ref, pb_ref))
    ]
    for copy in copies:
        copy.start()
    for copy in copies:
        copy.wait()


def panel_call(a):
    half = jax.ShapeDtypeStruct((a.shape[0] // 2, PANEL), F32)
    return pl.pallas_call(
        panel_kernel,
        in_specs=[pl.BlockSpec(memory_space=pltpu.HBM)],
        out_specs=[pl.BlockSpec(memory_space=pltpu.VMEM)] * 2,
        out_shape=[half, half],
        scratch_shapes=[pltpu.SemaphoreType.DMA((2,))],
        compiler_params=params(LARGE),
        name="panel",
    )(a)


def load_kernel(a_ref, blocks_ref, lower_ref, upper_ref, sem):
    copies = []
    for i in range(8):
        source = a_ref.at[:, i * WIDTH : (i + 1) * WIDTH]
        copies.append(pltpu.make_async_copy(source, blocks_ref.at[i], sem.at[i]))
        copies[i].start()
    for copy in copies:
        copy.wait()

    @pl.when(lax.axis_index("row") == 0)
    def _():
        for i, piece in enumerate((0, 3, 1, 2)):
            lower_ref[i] = blocks_ref[piece, :PANEL]
            upper_ref[i] = blocks_ref[piece + 4, :PANEL]


def load_call(a):
    scratch = [pltpu.SemaphoreType.DMA((8,))]
    keys = dict(scratch=scratch, mib=36, hbm=1, cost=cost_of(5))
    top = (4, PANEL, WIDTH)
    return small_call(load_kernel, [(8, a.shape[0], WIDTH), top, top], "load", a, **keys)


def split_kernel(lower_ref, upper_ref, *out_refs):
    core, _, _ = place()
    for i, out_ref in enumerate(out_refs):

        @pl.when(core == 0)
        def _(i=i, out_ref=out_ref):
            out_ref[...] = lower_ref[i]

        @pl.when(core != 0)
        def _(i=i, out_ref=out_ref):
            out_ref[...] = upper_ref[i]


def pick_kernel(mine_ref, far_ref, near_ref, diagonal_ref, out_ref):
    _, a0, _ = place()
    for at, ref in ((0, mine_ref), (far(0), far_ref), (near(0), near_ref), (diagonal(0), diagonal_ref)):

        @pl.when(a0 == at)
        def _(ref=ref):
            out_ref[...] = ref[...]


def pick_panel(pa, pb, a01, a03, a12, b01, b03, b32):
    x = lax.axis_index("col")
    upper = jnp.where(x == 0, pa[...], jnp.where(x == 1, a01[...], jnp.where(x == 2, a12[...], a03[...])))
    lower = jnp.where(x == 0, pb[...], jnp.where(x == 1, b01[...], jnp.where(x == 2, b32[...], b03[...])))
    return jnp.concatenate([upper, lower], axis=0)


def product_steps(flip, a_ref, lhs_ref, out_ref):
    half, a0, _ = place(flip)
    for i in range(4):
        high, low = split(a_ref[half * 4 + piece_at(a0, i)])
        both = dot3(lhs_ref[...], high)
        out_ref[i] = both[:PANEL] + both[PANEL:] + dot3(lhs_ref[:PANEL], low)


def product_first_kernel(a_ref, *refs):
    out_ref, lhs_ref, panel_ref, keep_ref, send_ref = refs[-5:]
    r = lax.axis_index("row")
    panel = pick_panel(*refs[:8])
    panel_ref[...] = panel
    flipped = panel.T
    high, low = split(flipped)
    lhs_ref[:PANEL] = high
    lhs_ref[PANEL:] = low
    gram = jnp.dot(flipped, panel, precision=HIGH, preferred_element_type=F32)
    top = jnp.where(r == 0, panel[:PANEL], 0.0)
    even = r & 1 == 0
    keep_ref[...] = jnp.where(even, gram, top)
    send_ref[...] = jnp.where(even, top, gram)
    product_steps(True, a_ref, lhs_ref, out_ref)


def product_second_kernel(a_ref, lhs_ref, out_ref):
    product_steps(False, a_ref, lhs_ref, out_ref)


def product_call(blocks, panels=None, lhs=None, after=()):
    rows = blocks.shape[1]
    w = ((4, PANEL, WIDTH), F32)
    if lhs is not None:
        return small_call(product_second_kernel, [w], "product_second", blocks, lhs, mib=24, cost=cost_of(1.5))[0]
    square = ((PANEL, PANEL), F32)
    shapes = [w, ((2 * PANEL, rows), BF16), ((rows, PANEL), F32), square, square]
    return small_call(product_first_kernel, shapes, "product_first", blocks, *panels, mib=24, cost=cost_of(2), after=after)


def spread(x, j):
    return jnp.broadcast_to(x[:, j : j + 1], (8, PANEL))


def tree_sum(terms):
    while len(terms) > 1:
        odd = [terms[-1]] if len(terms) % 2 else []
        terms = [p + q for p, q in zip(terms[::2], terms[1::2])] + odd
    return terms[0]


def chol_blocks(blocks):
    lane = lax.broadcasted_iota(jnp.int32, (8, PANEL), 1)
    sub = lax.broadcasted_iota(jnp.int32, (8, PANEL), 0)
    done = []
    for p in range(16):
        at = 8 * p
        rows = [jnp.broadcast_to(blocks[p][j : j + 1], (8, PANEL)) for j in range(8)]
        d = [[spread(rows[i], at + j) for j in range(i + 1)] for i in range(8)]
        t = [[None] * 8 for _ in range(8)]
        for k in range(8):
            r = lax.rsqrt(d[k][k])
            low = {i: d[i][k] * r for i in range(k + 1, 8)}
            for j in range(k):
                t[k][j] = t[k][j] * r
            t[k][k] = r
            for i in range(k + 1, 8):
                for j in range(k + 1, i + 1):
                    d[i][j] = d[i][j] - low[i] * low[j]
                for j in range(k + 1):
                    step = low[i] * t[k][j]
                    t[i][j] = -step if t[i][j] is None else t[i][j] - step
        inside = (lane >= at) & (lane < at + 8)
        rows = [jnp.where(inside, jnp.where(lane == at + j, 1.0, 0.0), rows[j]) for j in range(8)]
        y = []
        for i in range(8):
            terms = [t[i][j] * rows[j] for j in range(i + 1)]
            y.append(tree_sum(terms))
        out = y[0]
        for i in range(1, 8):
            out = jnp.where(sub == i, y[i], out)
        done.append(jnp.where(lane < at + 8, out, 0.0))
        if p == 15:
            break
        xs = []
        for k in range(8):
            terms = [t[i][k] * y[i] for i in range(k, 8)]
            xs.append(tree_sum(terms))
        for i in range(p + 1, 16):
            terms = [spread(blocks[i], at + k) * xs[k] for k in range(8)]
            blocks[i] = jnp.where(inside, 0.0, blocks[i]) - tree_sum(terms)
    return done


def inverse_blocks(blocks):
    lane = lax.broadcasted_iota(jnp.int32, (8, PANEL), 1)
    sub = lax.broadcasted_iota(jnp.int32, (8, PANEL), 0)
    for p in range(16):
        at = 8 * p
        rows = [jnp.broadcast_to(blocks[p][j : j + 1], (8, PANEL)) for j in range(8)]
        d = [[spread(rows[i], at + j) for j in range(8)] for i in range(8)]
        for k in range(8):
            r = 1.0 / d[k][k]
            row = [r if j == k else d[k][j] * r for j in range(8)]
            for i in range(8):
                if i != k:
                    m = d[i][k]
                    d[i] = [-(m * row[j]) if j == k else d[i][j] - m * row[j] for j in range(8)]
            d[k] = row
        inside = (lane >= at) & (lane < at + 8)
        rows = [jnp.where(inside, jnp.where(lane == at + j, 1.0, 0.0), rows[j]) for j in range(8)]
        xs = []
        for k in range(8):
            terms = [d[k][j] * rows[j] for j in range(8)]
            xs.append(tree_sum(terms))
        new = []
        for i in range(16):
            if i == p:
                out = xs[0]
                for k in range(1, 8):
                    out = jnp.where(sub == k, xs[k], out)
                new.append(out)
                continue
            terms = [spread(blocks[i], at + k) * xs[k] for k in range(8)]
            new.append(jnp.where(inside, 0.0, blocks[i]) - tree_sum(terms))
        blocks = new
    return blocks


def factor_kernel(g_ref, other_ref, out_ref):
    core, _, _ = place()
    gram = jnp.where(core == 0, g_ref[...], other_ref[...])
    blocks = chol_blocks([gram[8 * i : 8 * i + 8] for i in range(16)])
    for i in range(16):
        out_ref[8 * i : 8 * i + 8] = blocks[i]


def basis_kernel(linv_ref, g_ref, other_ref, panel_ref, out_ref):
    core, _, _ = place()
    top = jnp.where(core == 0, other_ref[...], g_ref[...])
    linv = linv_ref[...]
    nt = (((1,), (1,)), ((), ()))
    q_top = lax.dot_general(top, linv, nt, precision=HIGH, preferred_element_type=F32)
    lane = lax.broadcasted_iota(jnp.int32, (8, PANEL), 1)
    sub = lax.broadcasted_iota(jnp.int32, (8, PANEL), 0)
    blocks = [q_top[8 * i : 8 * i + 8] + jnp.where(lane == sub + 8 * i, 1.0, 0.0) for i in range(16)]
    kinv = jnp.concatenate(inverse_blocks(blocks), axis=0)
    tn = (((0,), (0,)), ((), ()))
    change = lax.dot_general(linv, kinv, tn, precision=HIGH, preferred_element_type=F32)
    basis = jnp.dot(panel_ref[...], change, precision=HIGH, preferred_element_type=F32)
    rest = basis[PANEL:]
    upper = basis[:PANEL] + jnp.where(lax.axis_index("row") == 0, kinv, 0.0)
    for part, begin, end in ((upper, 0, PANEL), (rest, PANEL, basis.shape[0])):
        high, low = split(part)
        out_ref[begin:end, 0:PANEL] = high
        out_ref[begin:end, PANEL : 2 * PANEL] = low
        out_ref[begin:end, 2 * PANEL :] = high


def cores_kernel(own_ref, got_ref, keep_ref, kept_ref, *out_refs):
    gram = keep_ref[...] + kept_ref[...]
    for i, out_ref in enumerate(out_refs):
        out_ref[:, :WIDTH] = own_ref[i] + got_ref[i]
        out_ref[:, WIDTH:] = gram


def first_kernel(e0, e1, e2, e3, w_ref, g_ref):
    total = e0[...] + e1[...] + e2[...] + e3[...]
    w_ref[...] = total[:, :WIDTH]
    g_ref[...] = total[:, WIDTH:]


def gram_kernel(g0, g1, g2, g3, *refs):
    out_ref = refs[-1]
    out_ref[...] = g0[...] + g1[...] + g2[...] + g3[...]


def piece_kernel(linv_ref, w0, w1, w2, w3, mine_ref, far_ref, near_ref, diagonal_ref, out_ref):
    _, _, b0 = place()
    w = w0[...] + w1[...] + w2[...] + w3[...]
    z = jnp.dot(linv_ref[...], w, precision=HIGH, preferred_element_type=F32)
    for at, ref in ((0, mine_ref), (far(0), far_ref), (near(0), near_ref), (diagonal(0), diagonal_ref)):

        @pl.when(b0 == at)
        def _(ref=ref):
            out_ref[...] = z + ref[...]


def update_kernel(count, begin, a_ref, v_ref, *refs):
    z_refs = refs[: 2 * count]
    out_ref, buffer, sem = refs[-3:]
    writes = []
    for i in range(2 * count):
        half, a0, _ = place(i >= count)
        piece = half * 4 + piece_at(a0, begin + i % count)
        cols = pl.ds(pl.multiple_of(piece * WIDTH, WIDTH), WIDTH)
        high, low = split(z_refs[i][...])
        stacked = jnp.concatenate([high, high, low], axis=0)
        buffer[i] = a_ref[piece] - dot3(v_ref[...], stacked)
        writes.append(pltpu.make_async_copy(buffer.at[i], out_ref.at[:, cols], sem.at[i]))
        writes[i].start()
    for write in writes:
        write.wait()


def update_call(blocks, v, mine, theirs, begin, out=None):
    _, rows, width = blocks.shape
    count = len(mine)
    vmem = pl.BlockSpec(memory_space=pltpu.VMEM)
    extra = () if out is None else (out,)
    return pl.pallas_call(
        functools.partial(update_kernel, count, begin),
        in_specs=[vmem] * (2 + 2 * count) + [pl.BlockSpec(memory_space=pltpu.HBM)] * len(extra),
        out_specs=pl.BlockSpec(memory_space=pltpu.HBM),
        out_shape=jax.ShapeDtypeStruct((rows, 8 * width), F32),
        input_output_aliases={2 + 2 * count: 0} if extra else {},
        scratch_shapes=[pltpu.VMEM((2 * count, rows, WIDTH), F32), pltpu.SemaphoreType.DMA((2 * count,))],
        compiler_params=params(32),
        name="update",
    )(blocks, v, *mine, *theirs, *extra)


def hold_kernel(*refs):
    pass


def hold(arrays, after):
    anywhere = pl.BlockSpec(memory_space=pl.ANY)
    return pl.pallas_call(
        hold_kernel,
        in_specs=[anywhere] * (len(arrays) + 1),
        out_specs=[anywhere] * len(arrays),
        out_shape=[jax.ShapeDtypeStruct(array.shape, array.dtype) for array in arrays],
        input_output_aliases={i: i for i in range(len(arrays))},
        compiler_params=params(2),
        name="hold",
    )(*arrays, after)


def on_device(a):
    rows = a.shape[0]
    pa, pb = panel_call(a)
    a01 = lax.ppermute(pa, "col", [(0, 1)])
    b03 = lax.ppermute(pb, "col", [(0, 3)])
    b01 = lax.ppermute(pb, "col", [(0, 1)])
    a03 = lax.ppermute(pa, "col", [(0, 3)])
    a12 = lax.ppermute(a01, "col", [(1, 2)])
    b32 = lax.ppermute(b03, "col", [(3, 2)])

    blocks, lower, upper = load_call(a)
    upper = lax.ppermute(upper, "row", [(0, 1)])
    tops = small_call(split_kernel, [(PANEL, WIDTH)] * 4, "split", lower, upper)
    got = [along(0, step, tops[i + 1], lambda a, b: a == 0 and b == 0) for i, step in enumerate(STEPS)]
    (top,) = small_call(pick_kernel, [(PANEL, WIDTH)], "pick", tops[0], *got)
    tops = [top] + [along(1, step, top, lambda a, b: b == 0) for step in STEPS]

    w_other, lhs, panel, keep, send_g = product_call(blocks, panels=(pa, pb, a01, a03, a12, b01, b03, b32))
    w_got, kept = swap(w_other), swap(send_g)
    w_own = product_call(blocks, lhs=lhs)
    e = small_call(cores_kernel, [(PANEL, WIDTH + PANEL)] * 4, "sum_cores", w_own, w_got, keep, kept)
    e = [e[0]] + [along(0, step, e[i + 1]) for i, step in enumerate(STEPS)]
    w, g = small_call(first_kernel, [(PANEL, WIDTH), (PANEL, PANEL)], "sum_first", *e)
    g = [g] + [along(1, step, g) for step in STEPS]
    w = [w] + [along(1, step, w) for step in STEPS]
    (g,) = small_call(gram_kernel, [(PANEL, PANEL)], "sum_gram", *g, cost=cost_of(3))
    g_other = swap(g)
    (linv,) = small_call(factor_kernel, [(PANEL, PANEL)], "factor", g, g_other, cost=cost_of(0.5))
    (z,) = small_call(piece_kernel, [(PANEL, WIDTH)], "piece", linv, *w, *tops)

    got = [along(0, step, z) for step in STEPS]
    theirs = swap(z)
    shapes = [((rows, 3 * PANEL), BF16)]
    (v,) = small_call(basis_kernel, shapes, "basis", linv, g, g_other, panel, mib=16, cost=cost_of(7))
    got = hold(got, v)
    others = [swap(piece) for piece in got]
    out = update_call(blocks, v, [z], [theirs], 0)
    return update_call(blocks, v, got, others, 1, out)


def solution(mesh):
    return jax.shard_map(
        on_device, mesh=mesh, in_specs=(P("row", "col"),), out_specs=P("row", "col"), check_vma=False
    )
```

```python
import functools

import jax
import jax.numpy as jnp
from jax import lax
from jax.experimental import pallas as pl
from jax.experimental.pallas import tpu as pltpu
from jax.sharding import PartitionSpec as P

PANEL = 128
WIDTH = 512
LARGE = 52
HIGH = lax.Precision.HIGHEST
F32 = jnp.float32
BF16 = jnp.bfloat16


def near(a):
    return a ^ 1


def far(a):
    return 3 - a


def diagonal(a):
    return a ^ 2


STEPS = (far, near, diagonal)


def row_of(z, y, c):
    return (z * 4 + y) * 2 + c


def axis_pairs(which, step, keep=lambda a, b: True):
    pairs = []
    for z in range(4):
        for y in range(4):
            for c in range(2):
                a, b = (z, y) if c else (y, z)
                if keep(a, b):
                    to = (step(a), b) if which == 0 else (a, step(b))
                    tz, ty = to if c else to[::-1]
                    pairs.append((row_of(z, y, c), row_of(tz, ty, c)))
    return pairs


def along(which, step, x, keep=lambda a, b: True):
    return lax.ppermute(x, "row", axis_pairs(which, step, keep))


def swap(x):
    return lax.ppermute(x, "row", [(r, r ^ 1) for r in range(32)])


def piece_at(a0, i):
    return jnp.where(i == 0, a0, jnp.where(i == 1, far(a0), jnp.where(i == 2, near(a0), a0 ^ 2)))


def dot3(x, y):
    return jnp.dot(x, y, preferred_element_type=F32)


def split(x):
    high = x.astype(BF16)
    return high, (x - high.astype(F32)).astype(BF16)


def params(mib):
    return pltpu.CompilerParams(vmem_limit_bytes=mib << 20)


def cost_of(microseconds):
    return pl.CostEstimate(flops=int(microseconds * 1.15e9), bytes_accessed=0, transcendentals=0)


def small_call(kernel, shapes, name, *args, scratch=(), mib=8, after=(), cost=None, hbm=0):
    vmem = pl.BlockSpec(memory_space=pltpu.VMEM)
    shapes = [shape if isinstance(shape[0], tuple) else (shape, F32) for shape in shapes]
    return pl.pallas_call(
        kernel,
        in_specs=[pl.BlockSpec(memory_space=pltpu.HBM)] * hbm
        + [vmem] * (len(args) - hbm)
        + [pl.BlockSpec(memory_space=pl.ANY)] * len(after),
        out_specs=[vmem] * len(shapes),
        out_shape=[jax.ShapeDtypeStruct(*shape) for shape in shapes],
        scratch_shapes=scratch,
        compiler_params=params(mib),
        cost_estimate=cost,
        name=name,
    )(*args, *after)


def place(flip=False):
    r = lax.axis_index("row")
    z, y, core = r >> 3, (r >> 1) & 3, r & 1
    if flip:
        core = 1 - core
    return core, jnp.where(core == 0, y, z), jnp.where(core == 0, z, y)


def panel_kernel(a_ref, pa_ref, pb_ref, sem):
    upper = pa_ref.shape[0]
    copies = [
        pltpu.make_async_copy(a_ref.at[:upper, :PANEL], pa_ref, sem.at[0]),
        pltpu.make_async_copy(a_ref.at[upper:, :PANEL], pb_ref, sem.at[1]),
    ]
    for copy in copies:
        copy.start()
    for copy in copies:
        copy.wait()


def panel_call(a):
    rows = a.shape[0]
    upper = rows * 7 // 12
    parts = [jax.ShapeDtypeStruct((count, PANEL), F32) for count in (upper, rows - upper)]
    return pl.pallas_call(
        panel_kernel,
        in_specs=[pl.BlockSpec(memory_space=pltpu.HBM)],
        out_specs=[pl.BlockSpec(memory_space=pltpu.VMEM)] * 2,
        out_shape=parts,
        scratch_shapes=[pltpu.SemaphoreType.DMA((2,))],
        compiler_params=params(LARGE),
        name="panel",
    )(a)


def load_kernel(a_ref, blocks_ref, lower_ref, upper_ref, sem):
    copies = []
    for i in range(8):
        source = a_ref.at[:, i * WIDTH : (i + 1) * WIDTH]
        copies.append(pltpu.make_async_copy(source, blocks_ref.at[i], sem.at[i]))
        copies[i].start()
    for copy in copies:
        copy.wait()

    @pl.when(lax.axis_index("row") == 0)
    def _():
        for i, piece in enumerate((0, 3, 1, 2)):
            lower_ref[i] = blocks_ref[piece, :PANEL]
            upper_ref[i] = blocks_ref[piece + 4, :PANEL]


def load_call(a):
    scratch = [pltpu.SemaphoreType.DMA((8,))]
    keys = dict(scratch=scratch, mib=36, hbm=1, cost=cost_of(5))
    top = (4, PANEL, WIDTH)
    return small_call(load_kernel, [(8, a.shape[0], WIDTH), top, top], "load", a, **keys)


def split_kernel(lower_ref, upper_ref, *out_refs):
    core, _, _ = place()
    for i, out_ref in enumerate(out_refs):

        @pl.when(core == 0)
        def _(i=i, out_ref=out_ref):
            out_ref[...] = lower_ref[i]

        @pl.when(core != 0)
        def _(i=i, out_ref=out_ref):
            out_ref[...] = upper_ref[i]


def pick_kernel(mine_ref, far_ref, near_ref, diagonal_ref, out_ref):
    _, a0, _ = place()
    for at, ref in ((0, mine_ref), (far(0), far_ref), (near(0), near_ref), (diagonal(0), diagonal_ref)):

        @pl.when(a0 == at)
        def _(ref=ref):
            out_ref[...] = ref[...]


def pick_panel(pa, pb, a01, a03, a12, b01, b03, b32):
    x = lax.axis_index("col")
    upper = jnp.where(x == 0, pa[...], jnp.where(x == 1, a01[...], jnp.where(x == 2, a12[...], a03[...])))
    lower = jnp.where(x == 0, pb[...], jnp.where(x == 1, b01[...], jnp.where(x == 2, b32[...], b03[...])))
    return jnp.concatenate([upper, lower], axis=0)


def product_steps(flip, a_ref, lhs_ref, out_ref):
    half, a0, _ = place(flip)
    for i in range(4):
        high, low = split(a_ref[half * 4 + piece_at(a0, i)])
        both = dot3(lhs_ref[...], high)
        out_ref[i] = both[:PANEL] + both[PANEL:] + dot3(lhs_ref[:PANEL], low)


def product_first_kernel(a_ref, *refs):
    out_ref, lhs_ref, panel_ref, keep_ref, send_ref = refs[-5:]
    r = lax.axis_index("row")
    panel = pick_panel(*refs[:8])
    panel_ref[...] = panel
    flipped = panel.T
    high, low = split(flipped)
    lhs_ref[:PANEL] = high
    lhs_ref[PANEL:] = low
    gram = jnp.dot(flipped, panel, precision=HIGH, preferred_element_type=F32)
    top = jnp.where(r == 0, panel[:PANEL], 0.0)
    even = r & 1 == 0
    keep_ref[...] = jnp.where(even, gram, top)
    send_ref[...] = jnp.where(even, top, gram)
    product_steps(True, a_ref, lhs_ref, out_ref)


def product_second_kernel(a_ref, lhs_ref, out_ref):
    product_steps(False, a_ref, lhs_ref, out_ref)


def product_call(blocks, panels=None, lhs=None, after=()):
    rows = blocks.shape[1]
    w = ((4, PANEL, WIDTH), F32)
    if lhs is not None:
        return small_call(product_second_kernel, [w], "product_second", blocks, lhs, mib=24, cost=cost_of(1.5))[0]
    square = ((PANEL, PANEL), F32)
    shapes = [w, ((2 * PANEL, rows), BF16), ((rows, PANEL), F32), square, square]
    return small_call(product_first_kernel, shapes, "product_first", blocks, *panels, mib=24, cost=cost_of(2), after=after)


def spread(x, j):
    return jnp.broadcast_to(x[:, j : j + 1], (8, PANEL))


def tree_sum(terms):
    while len(terms) > 1:
        odd = [terms[-1]] if len(terms) % 2 else []
        terms = [p + q for p, q in zip(terms[::2], terms[1::2])] + odd
    return terms[0]


def chol_blocks(blocks):
    lane = lax.broadcasted_iota(jnp.int32, (8, PANEL), 1)
    sub = lax.broadcasted_iota(jnp.int32, (8, PANEL), 0)
    done = []
    for p in range(16):
        at = 8 * p
        rows = [jnp.broadcast_to(blocks[p][j : j + 1], (8, PANEL)) for j in range(8)]
        d = [[spread(rows[i], at + j) for j in range(i + 1)] for i in range(8)]
        t = [[None] * 8 for _ in range(8)]
        for k in range(8):
            r = lax.rsqrt(d[k][k])
            low = {i: d[i][k] * r for i in range(k + 1, 8)}
            for j in range(k):
                t[k][j] = t[k][j] * r
            t[k][k] = r
            for i in range(k + 1, 8):
                for j in range(k + 1, i + 1):
                    d[i][j] = d[i][j] - low[i] * low[j]
                for j in range(k + 1):
                    step = low[i] * t[k][j]
                    t[i][j] = -step if t[i][j] is None else t[i][j] - step
        inside = (lane >= at) & (lane < at + 8)
        rows = [jnp.where(inside, jnp.where(lane == at + j, 1.0, 0.0), rows[j]) for j in range(8)]
        y = []
        for i in range(8):
            terms = [t[i][j] * rows[j] for j in range(i + 1)]
            y.append(tree_sum(terms))
        out = y[0]
        for i in range(1, 8):
            out = jnp.where(sub == i, y[i], out)
        done.append(jnp.where(lane < at + 8, out, 0.0))
        if p == 15:
            break
        xs = []
        for k in range(8):
            terms = [t[i][k] * y[i] for i in range(k, 8)]
            xs.append(tree_sum(terms))
        for i in range(p + 1, 16):
            terms = [spread(blocks[i], at + k) * xs[k] for k in range(8)]
            blocks[i] = jnp.where(inside, 0.0, blocks[i]) - tree_sum(terms)
    return done


def inverse_blocks(blocks):
    lane = lax.broadcasted_iota(jnp.int32, (8, PANEL), 1)
    sub = lax.broadcasted_iota(jnp.int32, (8, PANEL), 0)
    for p in range(16):
        at = 8 * p
        rows = [jnp.broadcast_to(blocks[p][j : j + 1], (8, PANEL)) for j in range(8)]
        d = [[spread(rows[i], at + j) for j in range(8)] for i in range(8)]
        for k in range(8):
            r = 1.0 / d[k][k]
            row = [r if j == k else d[k][j] * r for j in range(8)]
            for i in range(8):
                if i != k:
                    m = d[i][k]
                    d[i] = [-(m * row[j]) if j == k else d[i][j] - m * row[j] for j in range(8)]
            d[k] = row
        inside = (lane >= at) & (lane < at + 8)
        rows = [jnp.where(inside, jnp.where(lane == at + j, 1.0, 0.0), rows[j]) for j in range(8)]
        xs = []
        for k in range(8):
            terms = [d[k][j] * rows[j] for j in range(8)]
            xs.append(tree_sum(terms))
        new = []
        for i in range(16):
            if i == p:
                out = xs[0]
                for k in range(1, 8):
                    out = jnp.where(sub == k, xs[k], out)
                new.append(out)
                continue
            terms = [spread(blocks[i], at + k) * xs[k] for k in range(8)]
            new.append(jnp.where(inside, 0.0, blocks[i]) - tree_sum(terms))
        blocks = new
    return blocks


def factor_kernel(g_ref, other_ref, out_ref):
    core, _, _ = place()
    gram = jnp.where(core == 0, g_ref[...], other_ref[...])
    blocks = chol_blocks([gram[8 * i : 8 * i + 8] for i in range(16)])
    for i in range(16):
        out_ref[8 * i : 8 * i + 8] = blocks[i]


def basis_kernel(linv_ref, g_ref, other_ref, panel_ref, out_ref):
    core, _, _ = place()
    top = jnp.where(core == 0, other_ref[...], g_ref[...])
    linv = linv_ref[...]
    nt = (((1,), (1,)), ((), ()))
    q_top = lax.dot_general(top, linv, nt, precision=HIGH, preferred_element_type=F32)
    lane = lax.broadcasted_iota(jnp.int32, (8, PANEL), 1)
    sub = lax.broadcasted_iota(jnp.int32, (8, PANEL), 0)
    blocks = [q_top[8 * i : 8 * i + 8] + jnp.where(lane == sub + 8 * i, 1.0, 0.0) for i in range(16)]
    kinv = jnp.concatenate(inverse_blocks(blocks), axis=0)
    tn = (((0,), (0,)), ((), ()))
    change = lax.dot_general(linv, kinv, tn, precision=HIGH, preferred_element_type=F32)
    basis = jnp.dot(panel_ref[...], change, precision=HIGH, preferred_element_type=F32)
    rest = basis[PANEL:]
    upper = basis[:PANEL] + jnp.where(lax.axis_index("row") == 0, kinv, 0.0)
    for part, begin, end in ((upper, 0, PANEL), (rest, PANEL, basis.shape[0])):
        high, low = split(part)
        out_ref[begin:end, 0:PANEL] = high
        out_ref[begin:end, PANEL : 2 * PANEL] = low
        out_ref[begin:end, 2 * PANEL :] = high


def cores_kernel(own_ref, got_ref, keep_ref, kept_ref, *out_refs):
    gram = keep_ref[...] + kept_ref[...]
    for i, out_ref in enumerate(out_refs):
        out_ref[:, :WIDTH] = own_ref[i] + got_ref[i]
        out_ref[:, WIDTH:] = gram


def first_kernel(e0, e1, e2, e3, w_ref, g_ref):
    total = e0[...] + e1[...] + e2[...] + e3[...]
    w_ref[...] = total[:, :WIDTH]
    g_ref[...] = total[:, WIDTH:]


def gram_kernel(g0, g1, g2, g3, *refs):
    out_ref = refs[-1]
    out_ref[...] = g0[...] + g1[...] + g2[...] + g3[...]


def piece_kernel(linv_ref, w0, w1, w2, w3, mine_ref, far_ref, near_ref, diagonal_ref, out_ref):
    _, _, b0 = place()
    w = w0[...] + w1[...] + w2[...] + w3[...]
    z = jnp.dot(linv_ref[...], w, precision=HIGH, preferred_element_type=F32)
    for at, ref in ((0, mine_ref), (far(0), far_ref), (near(0), near_ref), (diagonal(0), diagonal_ref)):

        @pl.when(b0 == at)
        def _(ref=ref):
            out_ref[...] = z + ref[...]


def update_kernel(count, begin, a_ref, v_ref, *refs):
    z_refs = refs[: 2 * count]
    out_ref, buffer, sem = refs[-3:]
    writes = []
    for i in range(2 * count):
        half, a0, _ = place(i >= count)
        piece = half * 4 + piece_at(a0, begin + i % count)
        cols = pl.ds(pl.multiple_of(piece * WIDTH, WIDTH), WIDTH)
        high, low = split(z_refs[i][...])
        stacked = jnp.concatenate([high, high, low], axis=0)
        buffer[i] = a_ref[piece] - dot3(v_ref[...], stacked)
        writes.append(pltpu.make_async_copy(buffer.at[i], out_ref.at[:, cols], sem.at[i]))
        writes[i].start()
    for write in writes:
        write.wait()


def update_call(blocks, v, mine, theirs, begin, out=None):
    _, rows, width = blocks.shape
    count = len(mine)
    vmem = pl.BlockSpec(memory_space=pltpu.VMEM)
    extra = () if out is None else (out,)
    return pl.pallas_call(
        functools.partial(update_kernel, count, begin),
        in_specs=[vmem] * (2 + 2 * count) + [pl.BlockSpec(memory_space=pltpu.HBM)] * len(extra),
        out_specs=pl.BlockSpec(memory_space=pltpu.HBM),
        out_shape=jax.ShapeDtypeStruct((rows, 8 * width), F32),
        input_output_aliases={2 + 2 * count: 0} if extra else {},
        scratch_shapes=[pltpu.VMEM((2 * count, rows, WIDTH), F32), pltpu.SemaphoreType.DMA((2 * count,))],
        compiler_params=params(32),
        name="update",
    )(blocks, v, *mine, *theirs, *extra)


def hold_kernel(*refs):
    pass


def hold(arrays, after):
    anywhere = pl.BlockSpec(memory_space=pl.ANY)
    return pl.pallas_call(
        hold_kernel,
        in_specs=[anywhere] * (len(arrays) + 1),
        out_specs=[anywhere] * len(arrays),
        out_shape=[jax.ShapeDtypeStruct(array.shape, array.dtype) for array in arrays],
        input_output_aliases={i: i for i in range(len(arrays))},
        compiler_params=params(2),
        name="hold",
    )(*arrays, after)


def on_device(a):
    rows = a.shape[0]
    pa, pb = panel_call(a)
    a01 = lax.ppermute(pa, "col", [(0, 1)])
    b03 = lax.ppermute(pb, "col", [(0, 3)])
    b01 = lax.ppermute(pb, "col", [(0, 1)])
    a03 = lax.ppermute(pa, "col", [(0, 3)])
    a12 = lax.ppermute(a01, "col", [(1, 2)])
    b32 = lax.ppermute(b03, "col", [(3, 2)])

    blocks, lower, upper = load_call(a)
    upper = lax.ppermute(upper, "row", [(0, 1)])
    tops = small_call(split_kernel, [(PANEL, WIDTH)] * 4, "split", lower, upper)
    got = [along(0, step, tops[i + 1], lambda a, b: a == 0 and b == 0) for i, step in enumerate(STEPS)]
    (top,) = small_call(pick_kernel, [(PANEL, WIDTH)], "pick", tops[0], *got)
    tops = [top] + [along(1, step, top, lambda a, b: b == 0) for step in STEPS]

    w_other, lhs, panel, keep, send_g = product_call(blocks, panels=(pa, pb, a01, a03, a12, b01, b03, b32))
    w_got, kept = swap(w_other), swap(send_g)
    w_own = product_call(blocks, lhs=lhs)
    e = small_call(cores_kernel, [(PANEL, WIDTH + PANEL)] * 4, "sum_cores", w_own, w_got, keep, kept)
    e = [e[0]] + [along(0, step, e[i + 1]) for i, step in enumerate(STEPS)]
    w, g = small_call(first_kernel, [(PANEL, WIDTH), (PANEL, PANEL)], "sum_first", *e)
    g = [g] + [along(1, step, g) for step in STEPS]
    w = [w] + [along(1, step, w) for step in STEPS]
    (g,) = small_call(gram_kernel, [(PANEL, PANEL)], "sum_gram", *g, cost=cost_of(3))
    g_other = swap(g)
    (linv,) = small_call(factor_kernel, [(PANEL, PANEL)], "factor", g, g_other, cost=cost_of(0.5))
    (z,) = small_call(piece_kernel, [(PANEL, WIDTH)], "piece", linv, *w, *tops)

    got = [along(0, step, z) for step in STEPS]
    theirs = swap(z)
    shapes = [((rows, 3 * PANEL), BF16)]
    (v,) = small_call(basis_kernel, shapes, "basis", linv, g, g_other, panel, mib=16, cost=cost_of(7))
    got = hold(got, v)
    others = [swap(piece) for piece in got]
    out = update_call(blocks, v, [z], [theirs], 0)
    return update_call(blocks, v, got, others, 1, out)


def solution(mesh):
    return jax.shard_map(
        on_device, mesh=mesh, in_specs=(P("row", "col"),), out_specs=P("row", "col"), check_vma=False
    )
```
